32 devices in a mesh: grp: 4 (over y, core), blk: 8 (over z, x).
Axes of the slice: x: 2, y: 2, z: 4, core: 2. Of those that a mesh axis runs over, the one named last changes fastest.
Arguments:
- unlabeled: bfloat16 [16384, 1024], P('blk'), may hold values from -10 to 10
- labeled: bfloat16 [32768, 1024], P(('grp', 'blk')), may hold values from -5 to 5
- picks: int32 [128], replicated, may hold values from 0 to 16383, as said below
Outputs:
- nearest: float32 [16384], P('blk')
The draws below stay inside these ranges and needn't reach their ends.
Inputs may be any that keep to these rules, and one draw needn't show every extreme that they name: `picks`: indices may repeat; row 0 and row 16383 are always among them.
All inputs are finite; a program needn't handle non-finite values.
Results may differ from the reference program's by a relative error of at most 0.0003.
Values may be sent and summed in bfloat16 or wider, within the bound.
No kernel may reach another device: no remote copies, remote signals or barrier semaphores. Data moves between devices by JAX's collectives and lax.ppermute only.
A program may use at most 64 MiB of HBM per device.

```python
import jax
import jax.numpy as jnp
from jax import lax

D = 1024
U_DEV = 2048
L_DEV = 1024
STEPS = 2
PICKS = 128
UN = 16384
N_GRP = 4
N_BLK = 8


def labeled_row(base, index):
    sub = jax.random.fold_in(base, index)
    return jax.random.truncated_normal(sub, -5.0, 5.0, (D,), jnp.float32)


def pick_indices(key):
    sub = jax.random.fold_in(key, 37)
    key_raw, key_slot = jax.random.split(sub, 2)
    count = N_BLK * U_DEV
    raw = jax.random.randint(key_raw, (PICKS,), 0, count, jnp.int32)
    slots = jax.random.permutation(key_slot, PICKS)[:2]
    raw = raw.at[slots[0]].set(0)
    raw = raw.at[slots[1]].set(count - 1)
    return raw.astype(jnp.int32)


def unit_noise(sub, shape):
    return jax.random.truncated_normal(sub, -5.0, 5.0, shape, jnp.float32)


def draw_picks(key, part):
    return pick_indices(key)


def draw_labeled(key, part):
    base = jax.random.fold_in(key, 11)
    count = N_GRP * N_BLK * L_DEV
    indices = jnp.arange(count, dtype=jnp.int32)
    rows = jax.vmap(lambda index: labeled_row(base, index))(indices)
    return rows.astype(jnp.bfloat16)


def draw_unlabeled(key, part):
    base = jax.random.fold_in(key, 11)
    mixer = jax.random.fold_in(key, 23)
    keys = jax.random.split(mixer, 9)
    key_group, key_back, key_row, key_weight, key_noise = (keys[0], keys[1], keys[2], keys[3], keys[4])
    key_coin, key_target, key_close, key_near = (keys[5], keys[6], keys[7], keys[8])
    count = N_BLK * U_DEV
    indices = jnp.arange(count, dtype=jnp.int32)
    owner = indices // U_DEV
    group = jax.random.randint(key_group, (count,), 0, N_GRP, jnp.int32)
    back = jax.random.randint(key_back, (count,), 0, STEPS + 1, jnp.int32)
    within = jax.random.randint(key_row, (count,), 0, L_DEV, jnp.int32)
    source = (group * N_BLK + (owner - back) % N_BLK) * L_DEV + within
    partner = jax.vmap(lambda index: labeled_row(base, index))(source)
    weight = jax.random.uniform(key_weight, (count, 1), jnp.float32, 0.3, 0.9)
    noise = unit_noise(key_noise, (count, D))
    drawn = weight * partner + jnp.sqrt(1.0 - weight * weight) * noise
    picks = pick_indices(key)
    picked = jnp.any(indices[:, None] == picks[None, :], axis=1)
    coin = jax.random.randint(key_coin, (count,), 0, 4, jnp.int32)
    variant = (coin == 0) & jnp.logical_not(picked)
    target = picks[jax.random.randint(key_target, (count,), 0, PICKS, jnp.int32)]
    close = jax.random.uniform(key_close, (count, 1), jnp.float32, 0.9, 0.97)
    near_noise = unit_noise(key_near, (count, D))
    near = close * drawn[target] + jnp.sqrt(1.0 - close * close) * near_noise
    rows = jnp.where(variant[:, None], near, drawn)
    return rows.astype(jnp.bfloat16)


def setup_inputs(seed: int = 0) -> dict:
    seeds = jax.random.split(jax.random.key(seed), 4)
    unlabeled = draw_unlabeled(jax.random.fold_in(seeds[3], 71), 0)
    labeled = draw_labeled(jax.random.fold_in(seeds[3], 71), 0)
    picks = draw_picks(jax.random.fold_in(seeds[3], 71), 0)
    return dict(unlabeled=unlabeled, labeled=labeled, picks=picks)


def squares(rows):
    wide = rows.astype(jnp.float32)
    return jnp.sum(wide * wide, axis=1)


def least(rows, rows_sq, others):
    others_sq = squares(others)
    inner = jnp.dot(rows, others.T, preferred_element_type=jnp.float32)
    scaled = (rows_sq[:, None] + others_sq[None, :] - 2.0 * inner) / D
    return jnp.min(scaled, axis=1)


def reference(unlabeled, labeled, picks):
    blocks = labeled.reshape(N_GRP, N_BLK, L_DEV, D)
    rows = unlabeled.reshape(N_BLK, U_DEV, D)

    def per_block(index):
        mine = lax.dynamic_index_in_dim(rows, index, 0, keepdims=False)
        mine_sq = squares(mine)
        best = jnp.full((U_DEV,), jnp.inf, jnp.float32)
        for back in range(STEPS + 1):
            source = ((index - back) % N_BLK).astype(jnp.int32)
            pool = lax.dynamic_index_in_dim(blocks, source, 1, keepdims=False)
            for group in range(N_GRP):
                best = jnp.minimum(best, least(mine, mine_sq, pool[group]))
        return best

    labeled_min = lax.map(per_block, jnp.arange(N_BLK, dtype=jnp.int32)).reshape(UN)
    pick_rows = unlabeled[picks]
    pick_min = least(unlabeled, squares(unlabeled), pick_rows)
    return jnp.minimum(labeled_min, pick_min)
```

```python
import jax
import jax.numpy as jnp
from jax import lax
from jax.sharding import PartitionSpec as P

STEPS = 2
FORWARD = (176, 176)
BOTH = (160,)
AXES = ("grp", "blk")


def squares(rows):
    wide = rows.astype(jnp.float32)
    return jnp.sum(wide * wide, axis=1)


def least(rows, others, others_sq):
    inner = lax.dot_general(
        rows, others, (((1,), (1,)), ((), ())), preferred_element_type=jnp.float32
    )
    return jnp.min(others_sq[None, :] - 2.0 * inner, axis=1)


def body(n_grp, n_blk, unlabeled, labeled, picks):
    width = unlabeled.shape[1]
    rows_dev = unlabeled.shape[0]
    half = rows_dev // 2
    grp = lax.axis_index("grp")
    blk = lax.axis_index("blk")
    side, core = grp // 2, grp % 2
    odd = blk % 2 == 1

    def route(move):
        pairs = []
        for g in range(n_grp):
            for b in range(n_blk):
                to_g, to_b = move(g, b)
                pairs.append((g * n_blk + b, to_g * n_blk + to_b))
        return pairs

    def send(value, move):
        return lax.ppermute(value, AXES, route(move))

    back_two = lambda g, b: (g, (b - 2) % n_blk)
    ahead_two = lambda g, b: (g, (b + 2) % n_blk)
    ahead_one = lambda g, b: (g, (b + 1) % n_blk)
    swap_x = lambda g, b: (g, b ^ 1)
    swap_core = lambda g, b: (g ^ 1, b)
    swap_side = lambda g, b: (g ^ 2, b)

    start = core * half
    edge = sum(FORWARD)
    middle = half - 2 * edge
    first = start + side * (half - edge)
    sizes, starts = [], []
    at = first
    for size in FORWARD:
        sizes.append(size)
        starts.append(at)
        at = at + size
    at = start + edge
    for size in (middle // 2, middle - middle // 2):
        sizes.append(size)
        starts.append(at)
        at = at + size
    mine = [
        lax.dynamic_slice_in_dim(unlabeled, s, n, 0) for s, n in zip(starts, sizes)
    ]
    two = [send(chunk, back_two) for chunk in mine]
    partner = send(labeled, swap_core)
    one = [
        send(jnp.where(odd, own, got), swap_x) for own, got in zip(mine, two)
    ]
    n_fwd = len(FORWARD)
    two_side = [send(chunk, swap_side) for chunk in two[:n_fwd]]
    one_side = [send(chunk, swap_side) for chunk in one[:n_fwd]]

    labeled_sq = squares(labeled)
    partner_sq = squares(partner)

    def both(rows):
        return jnp.minimum(
            least(rows, labeled, labeled_sq), least(rows, partner, partner_sq)
        )

    def ordered(near, middle_part, far):
        near, far = jnp.concatenate(near), jnp.concatenate(far)
        lower = jnp.where(side == 0, near, far)
        upper = jnp.where(side == 0, far, near)
        return jnp.concatenate([lower] + middle_part + [upper])

    half_rows = lax.dynamic_slice_in_dim(unlabeled, start, half, 0)
    own_min = both(half_rows)
    two_min = [both(chunk) for chunk in two]
    one_min = [both(chunk) for chunk in one]
    two_far = [both(chunk) for chunk in two_side]
    one_far = [both(chunk) for chunk in one_side]
    two_all = ordered(two_min[:n_fwd], two_min[n_fwd:], two_far)
    one_all = ordered(one_min[:n_fwd], one_min[n_fwd:], one_far)

    share = picks.shape[0] // n_grp
    wanted = lax.dynamic_slice_in_dim(picks, grp * share, share, 0)
    local = wanted - blk * rows_dev
    owned = (local >= 0) & (local < rows_dev)
    taken = unlabeled[jnp.clip(local, 0, rows_dev - 1)]
    chosen = jnp.where(owned[:, None], taken, jnp.zeros_like(taken))
    hop = 1
    while hop < n_blk:
        chosen = chosen + send(chosen, lambda g, b: (g, b ^ hop))
        hop *= 2
    chosen = jnp.concatenate([chosen, send(chosen, swap_core)])
    own_min = jnp.minimum(own_min, least(half_rows, chosen, squares(chosen)))

    home = jnp.minimum(own_min, send(two_all, ahead_two))
    home = jnp.minimum(home, send(one_all, ahead_one))
    home = jnp.minimum(home, send(home, swap_side))
    home = (squares(half_rows) + home) / width
    other = send(home, swap_core)
    return jnp.concatenate(
        [jnp.where(core == 0, home, other), jnp.where(core == 0, other, home)]
    )


def solution(mesh):
    n_grp, n_blk = mesh.shape["grp"], mesh.shape["blk"]

    def run(unlabeled, labeled, picks):
        return body(n_grp, n_blk, unlabeled, labeled, picks)

    return jax.shard_map(
        run,
        mesh=mesh,
        in_specs=(P("blk", None), P(("grp", "blk"), None), P()),
        out_specs=P("blk"),
        check_vma=False,
    )
```

```python
import jax
import jax.numpy as jnp
from jax import lax
from jax.experimental import pallas as pl
from jax.experimental.pallas import tpu as pltpu
from jax.sharding import PartitionSpec as P


FORWARD = (176, 176)
AXES = ("grp", "blk")
TILE = 256
LANES = 128
KERNEL_BYTES = 16 * 2**20


def squares(rows):
    wide = rows.astype(jnp.float32)
    return jnp.sum(wide * wide, axis=1)


def after(value, *earlier):
    return lax.optimization_barrier((value, *earlier))[0]


def score_kernel(pieces, count, *refs):
    sources = refs[:count]
    near, far, near_half, far_half, out, rows, beyond, best, sems = refs[count:]
    copies = []
    at = 0
    for k, (source, offset, size) in enumerate(pieces):
        copies.append(
            pltpu.make_async_copy(
                sources[source].at[pl.ds(offset, size)],
                rows.at[pl.ds(at, size)],
                sems.at[k],
            )
        )
        at += size
    total = at
    other = pltpu.make_async_copy(far, beyond, sems.at[len(pieces)])
    for copy in copies:
        copy.start()
    other.start()
    best[...] = jnp.full_like(best, -jnp.inf)

    def against(block, halves):
        for t in range(0, block.shape[0], TILE):
            inner = lax.dot_general(
                rows[...],
                block[t : t + TILE, :],
                (((1,), (1,)), ((), ())),
                preferred_element_type=jnp.float32,
            )
            gain = inner - halves[:, t : t + TILE]
            top = gain[:, :LANES]
            for k in range(LANES, TILE, LANES):
                top = jnp.maximum(top, gain[:, k : k + LANES])
            best[0:total, :] = jnp.maximum(best[0:total, :], top)

    for copy in copies:
        copy.wait()
    against(near, near_half)
    other.wait()
    against(beyond, far_half)
    out[...] = jnp.max(best[...].T, axis=0, keepdims=True)


def score(chunks, near, far, near_half, far_half, pieces=None):
    if pieces is None:
        pieces = [(k, 0, chunk.shape[0]) for k, chunk in enumerate(chunks)]
    total = sum(piece[2] for piece in pieces)
    padded = -(-total // LANES) * LANES
    width = near.shape[1]
    block = near.shape[0]
    count = len(chunks)

    def kernel(*refs):
        score_kernel(pieces, count, *refs)

    hbm = pl.BlockSpec(memory_space=pl.ANY)
    vmem = pl.BlockSpec(memory_space=pltpu.VMEM)
    out = pl.pallas_call(
        kernel,
        out_shape=jax.ShapeDtypeStruct((1, padded), jnp.float32),
        in_specs=[hbm] * count + [vmem, hbm, vmem, vmem],
        out_specs=vmem,
        scratch_shapes=[
            pltpu.VMEM((total, width), jnp.bfloat16),
            pltpu.VMEM((block, width), jnp.bfloat16),
            pltpu.VMEM((padded, LANES), jnp.float32),
            pltpu.SemaphoreType.DMA((len(pieces) + 1,)),
        ],
        cost_estimate=pl.CostEstimate(
            flops=4 * total * block * width,
            bytes_accessed=2 * width * (total + 2 * block),
            transcendentals=0,
        ),
        compiler_params=pltpu.CompilerParams(vmem_limit_bytes=KERNEL_BYTES),
    )(*chunks, near, far, near_half, far_half)
    return out[0]


def body(n_grp, n_blk, unlabeled, labeled, picks):
    width = unlabeled.shape[1]
    rows_dev = unlabeled.shape[0]
    half = rows_dev // 2
    grp = lax.axis_index("grp")
    blk = lax.axis_index("blk")
    side, core = grp // 2, grp % 2
    odd = blk % 2 == 1

    def send(value, move):
        pairs = []
        for g in range(n_grp):
            for b in range(n_blk):
                to_g, to_b = move(g, b)
                pairs.append((g * n_blk + b, to_g * n_blk + to_b))
        return lax.ppermute(value, AXES, pairs)

    back_two = lambda g, b: (g, (b - 2) % n_blk)
    ahead_two = lambda g, b: (g, (b + 2) % n_blk)
    ahead_one = lambda g, b: (g, (b + 1) % n_blk)
    swap_x = lambda g, b: (g, b ^ 1)
    swap_core = lambda g, b: (g ^ 1, b)
    swap_side = lambda g, b: (g ^ 2, b)

    start = core * half
    edge = sum(FORWARD)
    middle = half - 2 * edge
    sizes, starts = [], []
    at = start + side * (half - edge)
    for size in FORWARD:
        sizes.append(size)
        starts.append(at)
        at = at + size
    at = start + edge
    for size in (middle // 2, middle - middle // 2):
        sizes.append(size)
        starts.append(at)
        at = at + size
    mine = [
        lax.dynamic_slice_in_dim(unlabeled, s, n, 0) for s, n in zip(starts, sizes)
    ]
    two = [send(chunk, back_two) for chunk in mine]
    far = send(labeled, swap_core)
    near_half = 0.5 * squares(labeled)
    far_half = send(near_half, swap_core)[None, :]
    near_half = near_half[None, :]

    def best(chunks, pieces=None):
        return score(chunks, labeled, far, near_half, far_half, pieces)

    half_rows = lax.dynamic_slice_in_dim(unlabeled, start, half, 0)
    rows_sq = squares(half_rows)
    quarter = half // 2

    def pick_share(*earlier):
        share = picks.shape[0] // n_grp
        wanted = lax.dynamic_slice_in_dim(picks, grp * share, share, 0)
        local = wanted - blk * rows_dev
        owned = (local >= 0) & (local < rows_dev)
        table = after(unlabeled, *earlier)
        taken = table[jnp.clip(local, 0, rows_dev - 1)]
        return jnp.where(owned[:, None], taken, jnp.zeros_like(taken))

    def chosen_for_x(k, *earlier):
        return jnp.where(odd, mine[k], after(two[k], *earlier))

    two_side = [send(two[k], swap_side) for k in range(2)]
    ship = chosen_for_x(0)
    one = [send(ship, swap_x)]
    own_low = best([after(half_rows, ship)], [(0, 0, quarter)])
    ship = chosen_for_x(1, own_low)
    one.append(send(ship, swap_x))
    chosen = pick_share(ship)
    first_round = send(chosen, swap_x)
    ship = chosen_for_x(2, chosen)
    one.append(send(ship, swap_x))
    one_side = [send(one[k], swap_side) for k in range(2)]
    own_high = best([after(half_rows, ship)], [(0, quarter, half - quarter)])
    z_edge = best([after(two[0], own_high), two[1]])
    ship = chosen_for_x(3, z_edge)
    one.append(send(ship, swap_x))
    chosen = chosen + after(first_round, ship)
    hop = 2
    while hop < n_blk:
        chosen = chosen + send(chosen, lambda g, b: (g, b ^ hop))
        hop *= 2
    z_rest = best([after(two_side[0], ship), two_side[1], two[2]])
    x_edge = best([after(two[3], z_rest), one[0], one[1]])
    x_rest = best([after(one[2], x_edge), one[3], one_side[0], one_side[1]])

    chosen = jnp.concatenate([chosen, send(chosen, swap_core)])
    inner = lax.dot_general(
        half_rows, chosen, (((1,), (1,)), ((), ())), preferred_element_type=jnp.float32
    )
    pick_best = jnp.max(inner - 0.5 * squares(chosen)[None, :], axis=1)

    def ordered(near, rest, beyond):
        lower = jnp.where(side == 0, near, beyond)
        upper = jnp.where(side == 0, beyond, near)
        return jnp.concatenate([lower, rest, upper])

    two_all = ordered(
        z_edge[:edge],
        jnp.concatenate([z_rest[edge : edge + sizes[2]], x_edge[: sizes[3]]]),
        z_rest[:edge],
    )
    one_all = ordered(
        x_edge[sizes[3] : sizes[3] + edge],
        x_rest[:middle],
        x_rest[middle : middle + edge],
    )
    own = jnp.concatenate([own_low, own_high])
    home = jnp.maximum(jnp.maximum(own, pick_best), send(two_all, ahead_two))
    home = jnp.maximum(home, send(one_all, ahead_one))
    home = jnp.maximum(home, send(home, swap_side))
    home = (rows_sq - 2.0 * home) / width
    other = send(home, swap_core)
    return jnp.concatenate(
        [jnp.where(core == 0, home, other), jnp.where(core == 0, other, home)]
    )


def solution(mesh):
    n_grp, n_blk = mesh.shape["grp"], mesh.shape["blk"]

    def run(unlabeled, labeled, picks):
        return body(n_grp, n_blk, unlabeled, labeled, picks)

    return jax.shard_map(
        run,
        mesh=mesh,
        in_specs=(P("blk", None), P(("grp", "blk"), None), P()),
        out_specs=P("blk"),
        check_vma=False,
    )
```

```python
import functools

import jax
import jax.numpy as jnp
from jax import lax
from jax.experimental import pallas as pl
from jax.experimental.pallas import tpu as pltpu
from jax.sharding import PartitionSpec as P


FORWARD = (144, 192)
BOTH = 2
AXES = ("grp", "blk")
TILE = 256
LANES = 128
PACK = 16
KERNEL_BYTES = 16 * 2**20


ANY = pl.BlockSpec(memory_space=pl.ANY)
VMEM = pl.BlockSpec(memory_space=pltpu.VMEM)
SMEM = pl.BlockSpec(memory_space=pltpu.SMEM)


def squares(rows):
    wide = rows.astype(jnp.float32)
    return jnp.sum(wide * wide, axis=1)


def aligned(at):
    return pl.multiple_of(at, PACK)


def cut_kernel(place, sizes, source, *refs):
    outs, sems = refs[:-1], refs[-1]
    copies = []
    for k, size in enumerate(sizes):
        rows = source.at[pl.ds(aligned(place(k)), size)]
        copies.append(pltpu.make_async_copy(rows, outs[k], sems.at[k]))
    for copy in copies:
        copy.start()
    for copy in copies:
        copy.wait()


def cut(source, place, sizes):
    width = source.shape[1]
    return pl.pallas_call(
        functools.partial(cut_kernel, place, sizes),
        out_shape=[jax.ShapeDtypeStruct((n, width), source.dtype) for n in sizes],
        in_specs=[ANY],
        out_specs=[VMEM] * len(sizes),
        scratch_shapes=[pltpu.SemaphoreType.DMA((len(sizes),))],
        cost_estimate=pl.CostEstimate(
            flops=0, bytes_accessed=4 * width * sum(sizes), transcendentals=0
        ),
        compiler_params=pltpu.CompilerParams(vmem_limit_bytes=KERNEL_BYTES),
    )(source)


def gather_kernel(share, picks, table, out, hold, pattern, sem):
    first = lax.axis_index("grp") * share
    base = lax.axis_index("blk") * table.shape[0]
    lane = lax.broadcasted_iota(jnp.int32, (1, share * PACK), 1)
    for p in range(share):
        local = picks[first + p] - base
        owned = (local >= 0) & (local < table.shape[0])
        row = jnp.clip(local, 0, table.shape[0] - 1)
        within = row & (PACK - 1)
        copy = pltpu.make_async_copy(
            table.at[pl.ds(aligned(row - within), PACK)],
            hold.at[pl.ds(p * PACK, PACK)],
            sem,
        )
        copy.start()
        spot = jnp.where(owned, p * PACK + within, -1)
        pattern[p : p + 1, :] = jnp.where(lane == spot, 1.0, 0.0)
    pltpu.make_async_copy(table.at[pl.ds(0, share * PACK)], hold, sem).wait()
    taken = jnp.dot(
        pattern[...].astype(hold.dtype), hold[...], preferred_element_type=jnp.float32
    )
    out[...] = taken.astype(out.dtype)


def gather(picks, table, share):
    width = table.shape[1]
    return pl.pallas_call(
        functools.partial(gather_kernel, share),
        out_shape=jax.ShapeDtypeStruct((share, width), table.dtype),
        in_specs=[SMEM, ANY],
        out_specs=VMEM,
        scratch_shapes=[
            pltpu.VMEM((share * PACK, width), table.dtype),
            pltpu.VMEM((share, share * PACK), jnp.float32),
            pltpu.SemaphoreType.DMA,
        ],
        cost_estimate=pl.CostEstimate(
            flops=2 * share * share * PACK * width,
            bytes_accessed=2 * share * PACK * width,
            transcendentals=0,
        ),
        compiler_params=pltpu.CompilerParams(vmem_limit_bytes=KERNEL_BYTES),
    )(picks, table)


def score_kernel(sizes, lead, picked, *refs):
    sources = refs[: len(sizes)]
    refs = list(refs[len(sizes) :])
    near, far, near_half, far_half = refs[:4]
    extra = refs[4:6] if picked else ()
    out, rows, beyond, best, sems = refs[-5:]
    copies = []
    at = 0
    for k, size in enumerate(sizes):
        copies.append(
            pltpu.make_async_copy(sources[k], rows.at[pl.ds(at, size)], sems.at[k])
        )
        at += size
    total, main = at, sum(sizes[:lead])
    other = pltpu.make_async_copy(far, beyond, sems.at[len(sizes)])
    for copy in copies:
        copy.start()
    other.start()
    best[...] = jnp.full_like(best, -jnp.inf)

    def against(block, halves, tile, count):
        for t in range(0, block.shape[0], tile):
            inner = lax.dot_general(
                rows[0:count, :],
                block[t : t + tile, :],
                (((1,), (1,)), ((), ())),
                preferred_element_type=jnp.float32,
            )
            gain = inner - halves[:, t : t + tile]
            reach = min(tile, LANES)
            top = gain[:, :reach]
            for k in range(LANES, tile, LANES):
                top = jnp.maximum(top, gain[:, k : k + LANES])
            best[0:count, 0:reach] = jnp.maximum(best[0:count, 0:reach], top)

    for copy in copies[:lead]:
        copy.wait()
    against(near, near_half, TILE, main)
    other.wait()
    against(beyond, far_half, TILE, main)
    for copy in copies[lead:]:
        copy.wait()
    if picked:
        against(extra[0], extra[1], extra[0].shape[0], total)
    out[...] = jnp.max(best[...].T, axis=0, keepdims=True)


def score(chunks, near, far, near_half, far_half, only=(), picked=()):
    sizes = [chunk.shape[0] for chunk in (*chunks, *only)]
    main = sum(chunk.shape[0] for chunk in chunks)
    total = sum(sizes)
    padded = -(-total // LANES) * LANES
    width = near.shape[1]
    block = near.shape[0]
    out = pl.pallas_call(
        functools.partial(score_kernel, sizes, len(chunks), bool(picked)),
        out_shape=jax.ShapeDtypeStruct((1, padded), jnp.float32),
        in_specs=[ANY] * len(sizes) + [VMEM, ANY, VMEM, VMEM] + [VMEM] * len(picked),
        out_specs=VMEM,
        scratch_shapes=[
            pltpu.VMEM((total, width), jnp.bfloat16),
            pltpu.VMEM((block, width), jnp.bfloat16),
            pltpu.VMEM((padded, LANES), jnp.float32),
            pltpu.SemaphoreType.DMA((len(sizes) + 1,)),
        ],
        cost_estimate=pl.CostEstimate(
            flops=4 * main * block * width,
            bytes_accessed=2 * width * (total + 2 * block),
            transcendentals=0,
        ),
        compiler_params=pltpu.CompilerParams(vmem_limit_bytes=KERNEL_BYTES),
    )(*chunks, *only, near, far, near_half, far_half, *picked)
    return out[0]


def body(n_grp, n_blk, unlabeled, labeled, picks):
    width = unlabeled.shape[1]
    rows_dev = unlabeled.shape[0]
    half = rows_dev // 2
    grp = lax.axis_index("grp")
    side, core = grp // 2, grp % 2
    odd = lax.axis_index("blk") % 2 == 1

    def send(value, move):
        pairs = []
        for g in range(n_grp):
            for b in range(n_blk):
                to_g, to_b = move(g, b)
                pairs.append((g * n_blk + b, to_g * n_blk + to_b))
        return lax.ppermute(value, AXES, pairs)

    back_two = lambda g, b: (g, (b - 2) % n_blk)
    ahead_two = lambda g, b: (g, (b + 2) % n_blk)
    ahead_one = lambda g, b: (g, (b + 1) % n_blk)
    swap_x = lambda g, b: (g, b ^ 1)
    swap_core = lambda g, b: (g ^ 1, b)
    swap_side = lambda g, b: (g ^ 2, b)
    swap_both = lambda g, b: (g ^ 3, b)

    edge = sum(FORWARD)
    middle = half - 2 * edge
    rest = [middle - middle // BOTH // PACK * PACK * (BOTH - 1)]
    rest += [middle // BOTH // PACK * PACK] * (BOTH - 1)

    def half_start():
        return (lax.axis_index("grp") % 2) * half

    def edge_start(k):
        far_side = lax.axis_index("grp") // 2
        return half_start() + far_side * (half - edge) + sum(FORWARD[:k])

    def rest_start(k):
        return half_start() + edge + sum(rest[:k])

    def far_edge():
        near_side = 1 - lax.axis_index("grp") // 2
        return half_start() + near_side * (half - edge)

    mine = list(cut(unlabeled, edge_start, list(FORWARD)))
    *between, beyond = cut(
        unlabeled, lambda k: rest_start(k) if k < BOTH else far_edge(), rest + [edge]
    )
    mine += between
    two = [send(chunk, back_two) for chunk in mine]
    far = send(labeled, swap_core)
    near_half = 0.5 * squares(labeled)
    far_half = send(near_half, swap_core)[None, :]
    near_half = near_half[None, :]

    def best(chunks, *more):
        return score(chunks, labeled, far, near_half, far_half, *more)

    def for_x(k):
        return jnp.where(odd, mine[k], two[k])

    one = [send(for_x(k), swap_x) for k in range(4)]
    two_side = [send(two[k], swap_side) for k in range(2)]
    one_side = [send(one[k], swap_side) for k in range(2)]

    own_a = best(mine)
    z_edge = best(two[:2])
    mid = best(two_side + two[2:] + one[:2])
    x_rest = best(one[2:] + one_side)

    chosen = gather(picks, unlabeled, picks.shape[0] // n_grp)
    hop = 1
    while hop < n_blk:
        chosen = chosen + send(chosen, lambda g, b: (g, b ^ hop))
        hop *= 2
    chosen = jnp.concatenate([chosen, send(chosen, swap_core)])
    chosen_half = 0.5 * squares(chosen)[None, :]
    own_b = best([beyond], mine, (chosen, chosen_half))

    def ordered(near, between, beyond):
        lower = jnp.where(side == 0, near, beyond)
        upper = jnp.where(side == 0, beyond, near)
        return jnp.concatenate([lower, between, upper])

    two_all = ordered(z_edge[:edge], mid[edge : edge + middle], mid[:edge])
    from_two = send(two_all, ahead_two)
    mid_later, _ = lax.optimization_barrier((mid, two_all))
    own_near = jnp.maximum(own_a[: edge + middle], own_b[edge:half])
    own_all = ordered(own_near[:edge], own_near[edge:], own_b[:edge])
    at = edge + middle
    one_all = ordered(
        mid_later[at : at + edge], x_rest[:middle], x_rest[middle : middle + edge]
    )
    from_one = send(one_all, ahead_one)
    rows_sq = squares(unlabeled)
    home = jnp.maximum(own_all, from_two)
    home = jnp.maximum(home, from_one)
    mine_best = jnp.maximum(home, send(home, swap_side))
    other_best = jnp.maximum(send(home, swap_core), send(home, swap_both))
    top = jnp.concatenate(
        [
            jnp.where(core == 0, mine_best, other_best),
            jnp.where(core == 0, other_best, mine_best),
        ]
    )
    return (rows_sq - 2.0 * top) / width


def solution(mesh):
    n_grp, n_blk = mesh.shape["grp"], mesh.shape["blk"]

    def run(unlabeled, labeled, picks):
        return body(n_grp, n_blk, unlabeled, labeled, picks)

    return jax.shard_map(
        run,
        mesh=mesh,
        in_specs=(P("blk", None), P(("grp", "blk"), None), P()),
        out_specs=P("blk"),
        check_vma=False,
    )
```

```python
import functools

import jax
import jax.numpy as jnp
from jax import lax
from jax.experimental import pallas as pl
from jax.experimental.pallas import tpu as pltpu
from jax.sharding import PartitionSpec as P


FORWARD = (144, 192)
BOTH = 2
AXES = ("grp", "blk")
TILE = 256
LANES = 128
PACK = 16
KERNEL_BYTES = 16 * 2**20
PICKED_BYTES = 16 * 2**20


ANY = pl.BlockSpec(memory_space=pl.ANY)
VMEM = pl.BlockSpec(memory_space=pltpu.VMEM)
SMEM = pl.BlockSpec(memory_space=pltpu.SMEM)


def squares(rows):
    wide = rows.astype(jnp.float32)
    return jnp.sum(wide * wide, axis=1)


def aligned(at):
    return pl.multiple_of(at, PACK)


def cut_kernel(place, sizes, source, *refs):
    outs, sems = refs[:-1], refs[-1]
    copies = []
    for k, size in enumerate(sizes):
        rows = source.at[pl.ds(aligned(place(k)), size)]
        copies.append(pltpu.make_async_copy(rows, outs[k], sems.at[k]))
    for copy in copies:
        copy.start()
    for copy in copies:
        copy.wait()


def cut(source, place, sizes):
    width = source.shape[1]
    return pl.pallas_call(
        functools.partial(cut_kernel, place, sizes),
        out_shape=[jax.ShapeDtypeStruct((n, width), source.dtype) for n in sizes],
        in_specs=[ANY],
        out_specs=[VMEM] * len(sizes),
        scratch_shapes=[pltpu.SemaphoreType.DMA((len(sizes),))],
        cost_estimate=pl.CostEstimate(
            flops=0, bytes_accessed=4 * width * sum(sizes), transcendentals=0
        ),
        compiler_params=pltpu.CompilerParams(vmem_limit_bytes=KERNEL_BYTES),
    )(source)


def gather_kernel(share, picks, table, out, hold, pattern, sem):
    first = lax.axis_index("grp") * share
    base = lax.axis_index("blk") * table.shape[0]
    lane = lax.broadcasted_iota(jnp.int32, (1, share * PACK), 1)
    for p in range(share):
        local = picks[first + p] - base
        owned = (local >= 0) & (local < table.shape[0])
        row = jnp.clip(local, 0, table.shape[0] - 1)
        within = row & (PACK - 1)
        copy = pltpu.make_async_copy(
            table.at[pl.ds(aligned(row - within), PACK)],
            hold.at[pl.ds(p * PACK, PACK)],
            sem,
        )
        copy.start()
        spot = jnp.where(owned, p * PACK + within, -1)
        pattern[p : p + 1, :] = jnp.where(lane == spot, 1.0, 0.0)
    pltpu.make_async_copy(table.at[pl.ds(0, share * PACK)], hold, sem).wait()
    taken = jnp.dot(
        pattern[...].astype(hold.dtype), hold[...], preferred_element_type=jnp.float32
    )
    out[...] = taken.astype(out.dtype)


def gather(picks, table, share):
    width = table.shape[1]
    return pl.pallas_call(
        functools.partial(gather_kernel, share),
        out_shape=jax.ShapeDtypeStruct((share, width), table.dtype),
        in_specs=[SMEM, ANY],
        out_specs=VMEM,
        scratch_shapes=[
            pltpu.VMEM((share * PACK, width), table.dtype),
            pltpu.VMEM((share, share * PACK), jnp.float32),
            pltpu.SemaphoreType.DMA,
        ],
        cost_estimate=pl.CostEstimate(
            flops=2 * share * share * PACK * width,
            bytes_accessed=2 * share * PACK * width,
            transcendentals=0,
        ),
        compiler_params=pltpu.CompilerParams(vmem_limit_bytes=KERNEL_BYTES),
    )(picks, table)


def score_kernel(sizes, *refs):
    sources = refs[: len(sizes)]
    near, far, near_half, far_half, out, rows, beyond, best, sems = refs[len(sizes) :]
    copies = []
    at = 0
    for k, size in enumerate(sizes):
        copies.append(
            pltpu.make_async_copy(sources[k], rows.at[pl.ds(at, size)], sems.at[k])
        )
        at += size
    total = at
    other = pltpu.make_async_copy(far, beyond, sems.at[len(sizes)])
    for copy in copies:
        copy.start()
    other.start()
    best[...] = jnp.full_like(best, -jnp.inf)

    def against(block, halves):
        for t in range(0, block.shape[0], TILE):
            inner = lax.dot_general(
                rows[...],
                block[t : t + TILE, :],
                (((1,), (1,)), ((), ())),
                preferred_element_type=jnp.float32,
            )
            gain = inner - halves[:, t : t + TILE]
            top = gain[:, :LANES]
            for k in range(LANES, TILE, LANES):
                top = jnp.maximum(top, gain[:, k : k + LANES])
            best[0:total, :] = jnp.maximum(best[0:total, :], top)

    for copy in copies:
        copy.wait()
    against(near, near_half)
    other.wait()
    against(beyond, far_half)
    out[...] = jnp.max(best[...].T, axis=0, keepdims=True)


def score(chunks, near, far, near_half, far_half):
    sizes = [chunk.shape[0] for chunk in chunks]
    total = sum(sizes)
    padded = -(-total // LANES) * LANES
    width = near.shape[1]
    block = near.shape[0]
    out = pl.pallas_call(
        functools.partial(score_kernel, sizes),
        out_shape=jax.ShapeDtypeStruct((1, padded), jnp.float32),
        in_specs=[ANY] * len(sizes) + [VMEM, ANY, VMEM, VMEM],
        out_specs=VMEM,
        scratch_shapes=[
            pltpu.VMEM((total, width), jnp.bfloat16),
            pltpu.VMEM((block, width), jnp.bfloat16),
            pltpu.VMEM((padded, LANES), jnp.float32),
            pltpu.SemaphoreType.DMA((len(sizes) + 1,)),
        ],
        cost_estimate=pl.CostEstimate(
            flops=4 * total * block * width,
            bytes_accessed=2 * width * (total + 2 * block),
            transcendentals=0,
        ),
        compiler_params=pltpu.CompilerParams(vmem_limit_bytes=KERNEL_BYTES),
    )(*chunks, near, far, near_half, far_half)
    return out[0]


def picked_kernel(sizes, *refs):
    sources = refs[: len(sizes)]
    chosen, out, rows, best, sems = refs[len(sizes) :]
    copies = []
    at = 0
    for k, size in enumerate(sizes):
        copies.append(
            pltpu.make_async_copy(sources[k], rows.at[pl.ds(at, size)], sems.at[k])
        )
        at += size
    for copy in copies:
        copy.start()
    best[...] = jnp.full_like(best, -jnp.inf)
    wide = chosen[...].astype(jnp.float32)
    half = 0.5 * jnp.sum((wide * wide).T, axis=0, keepdims=True)
    for copy in copies:
        copy.wait()
    inner = lax.dot_general(
        rows[...],
        chosen[...],
        (((1,), (1,)), ((), ())),
        preferred_element_type=jnp.float32,
    )
    best[:, 0 : chosen.shape[0]] = inner - half
    out[...] = jnp.max(best[...].T, axis=0, keepdims=True)


def score_picked(chunks, chosen):
    sizes = [chunk.shape[0] for chunk in chunks]
    total = sum(sizes)
    count, width = chosen.shape
    out = pl.pallas_call(
        functools.partial(picked_kernel, sizes),
        out_shape=jax.ShapeDtypeStruct((1, total), jnp.float32),
        in_specs=[ANY] * len(sizes) + [VMEM],
        out_specs=VMEM,
        scratch_shapes=[
            pltpu.VMEM((total, width), jnp.bfloat16),
            pltpu.VMEM((total, LANES), jnp.float32),
            pltpu.SemaphoreType.DMA((len(sizes),)),
        ],
        cost_estimate=pl.CostEstimate(
            flops=2 * total * count * width,
            bytes_accessed=2 * width * (total + count),
            transcendentals=0,
        ),
        compiler_params=pltpu.CompilerParams(vmem_limit_bytes=PICKED_BYTES),
    )(*chunks, chosen)
    return out[0]


def body(n_grp, n_blk, unlabeled, labeled, picks):
    width = unlabeled.shape[1]
    rows_dev = unlabeled.shape[0]
    half = rows_dev // 2
    grp = lax.axis_index("grp")
    side, core = grp // 2, grp % 2
    odd = lax.axis_index("blk") % 2 == 1

    def send(value, move):
        pairs = []
        for g in range(n_grp):
            for b in range(n_blk):
                to_g, to_b = move(g, b)
                pairs.append((g * n_blk + b, to_g * n_blk + to_b))
        return lax.ppermute(value, AXES, pairs)

    back_two = lambda g, b: (g, (b - 2) % n_blk)
    ahead_two = lambda g, b: (g, (b + 2) % n_blk)
    ahead_one = lambda g, b: (g, (b + 1) % n_blk)
    swap_x = lambda g, b: (g, b ^ 1)
    swap_core = lambda g, b: (g ^ 1, b)
    swap_side = lambda g, b: (g ^ 2, b)
    swap_both = lambda g, b: (g ^ 3, b)

    edge = sum(FORWARD)
    middle = half - 2 * edge
    rest = [middle - middle // BOTH // PACK * PACK * (BOTH - 1)]
    rest += [middle // BOTH // PACK * PACK] * (BOTH - 1)

    def half_start():
        return (lax.axis_index("grp") % 2) * half

    def edge_start(k):
        far_side = lax.axis_index("grp") // 2
        return half_start() + far_side * (half - edge) + sum(FORWARD[:k])

    def rest_start(k):
        return half_start() + edge + sum(rest[:k])

    def far_edge():
        near_side = 1 - lax.axis_index("grp") // 2
        return half_start() + near_side * (half - edge)

    mine = list(cut(unlabeled, edge_start, list(FORWARD)))
    *between, beyond = cut(
        unlabeled, lambda k: rest_start(k) if k < BOTH else far_edge(), rest + [edge]
    )
    mine += between
    two = [send(chunk, back_two) for chunk in mine]
    far = send(labeled, swap_core)
    near_half = 0.5 * squares(labeled)
    far_half = send(near_half, swap_core)[None, :]
    near_half = near_half[None, :]

    def best(chunks):
        return score(chunks, labeled, far, near_half, far_half)

    def for_x(k):
        return jnp.where(odd, mine[k], two[k])

    one = [send(for_x(k), swap_x) for k in range(4)]
    two_side = [send(two[k], swap_side) for k in range(2)]
    one_side = [send(one[k], swap_side) for k in range(2)]

    own_a = best(mine)
    own_c = best([beyond])
    z_edge = best(two[:2])
    mid = best(two_side + two[2:] + one[:2])
    x_rest = best(one[2:] + one_side)

    chosen = gather(picks, unlabeled, picks.shape[0] // n_grp)
    hop = 1
    while hop < n_blk:
        chosen = chosen + send(chosen, lambda g, b: (g, b ^ hop))
        hop *= 2
    chosen = jnp.concatenate([chosen, send(chosen, swap_core)])
    picked = score_picked(mine + [beyond], chosen)

    def ordered(near, between, beyond):
        lower = jnp.where(side == 0, near, beyond)
        upper = jnp.where(side == 0, beyond, near)
        return jnp.concatenate([lower, between, upper])

    two_all = ordered(z_edge[:edge], mid[edge : edge + middle], mid[:edge])
    from_two = send(two_all, ahead_two)
    mid_later, _ = lax.optimization_barrier((mid, two_all))
    own_near = jnp.concatenate([own_a[: edge + middle], own_c[:edge]])
    own_near = jnp.maximum(own_near, picked)
    own_all = ordered(own_near[:edge], own_near[edge:-edge], own_near[-edge:])
    at = edge + middle
    one_all = ordered(
        mid_later[at : at + edge], x_rest[:middle], x_rest[middle : middle + edge]
    )
    from_one = send(one_all, ahead_one)
    rows_sq = squares(unlabeled)
    home = jnp.maximum(own_all, from_two)
    home = jnp.maximum(home, from_one)
    mine_best = jnp.maximum(home, send(home, swap_side))
    other_best = jnp.maximum(send(home, swap_core), send(home, swap_both))
    top = jnp.concatenate(
        [
            jnp.where(core == 0, mine_best, other_best),
            jnp.where(core == 0, other_best, mine_best),
        ]
    )
    return (rows_sq - 2.0 * top) / width


def solution(mesh):
    n_grp, n_blk = mesh.shape["grp"], mesh.shape["blk"]

    def run(unlabeled, labeled, picks):
        return body(n_grp, n_blk, unlabeled, labeled, picks)

    return jax.shard_map(
        run,
        mesh=mesh,
        in_specs=(P("blk", None), P(("grp", "blk"), None), P()),
        out_specs=P("blk"),
        check_vma=False,
    )
```
